128 devices in a mesh: gx: 8 (over x, core), gy: 16 (over z, y).
Axes of the slice: x: 4, y: 4, z: 4, core: 2. Of those that a mesh axis runs over, the one named last changes fastest.
Arguments:
- upstream: bfloat16 [65536, 256], P(('gx', 'gy')), may hold values from -6 to 6
- saved_hilbert: bfloat16 [65536, 256], P(('gx', 'gy')), may hold values from -40 to 40
- saved_morton: bfloat16 [65536, 256], P(('gx', 'gy')), may hold values from -40 to 40
- gains: float32 [2, 256], replicated, may hold values from 0.1 to 1.9
- w_qkv: bfloat16 [2, 256, 768], replicated, may hold values from -4 to 4
- w_out: bfloat16 [2, 256, 256], replicated, may hold values from -0.375 to 0.375
- hilbert_tiles: int32 [512], replicated, may hold values from 0 to 511, as said below
- morton_tiles: int32 [512], replicated, may hold values from 0 to 511, as said below
Outputs:
- input_grad: bfloat16 [65536, 256], P(('gx', 'gy'))
- qkv_weight_grad: float32 [2, 256, 768], P(None, 'gy')
- out_weight_grad: float32 [2, 256, 256], P(None, 'gy')
- gain_grad: float32 [2, 256], P(None, 'gy')
The draws below stay inside these ranges and needn't reach their ends.
Inputs may be any that keep to these rules, and one draw needn't show every extreme that they name: `hilbert_tiles`: A permutation of the tile numbers. Tile t is stored on device t // 4 and position j lies on device j // 4, devices numbered gx-major; every tile stays at the same gx index; from one device to another go at most 2 tiles, and some pair of devices reaches 2; counts differ between pairs. `morton_tiles`: A permutation of the tile numbers, devices numbered as for hilbert_tiles; every tile stays at the same gy index; from one device to another go at most 2 tiles, and some pair of devices reaches 2; counts differ between pairs.
All inputs are finite; a program needn't handle non-finite values.
Results may differ from the reference program's by a relative error of at most 0.02.
The reference program's roundings to bfloat16 on the way (of `hidden`, `qkv`, `attended`, `out_grad` and `qkv_grad`) count: a program that leaves them out, or rounds other values in their place, can miss the bound.
Values may be sent and summed in bfloat16 or wider, within the bound.
A program may use at most 128 MiB of HBM per device.

```python
import jax
import jax.numpy as jnp
from jax import lax

C = 256
HEADS = 16
TILE = 128
PATCH = 256
BLOCKS = 2
TILES_DEV = 4
CAPY = 2
CAPX = 2
TILES = 512
POINTS = 65536
N_GX = 8
N_GY = 16


def tile_order(key, groups, size, tiles, capacity, first, second):

    def one_group(group_key):
        keys = jax.random.split(group_key, 4)
        values = jnp.repeat(jnp.arange(size, dtype=jnp.int32), capacity)
        ranks = jnp.tile(jnp.arange(capacity, dtype=jnp.int32), size)
        dropped = (values == second) | (values == first) & (ranks == 0)
        mixed = jax.random.permutation(keys[1], size * capacity).astype(jnp.int32)
        values_mixed = values[mixed]
        dropped_mixed = dropped[mixed].astype(jnp.int32)
        keep = jnp.argsort(dropped_mixed, stable=True).astype(jnp.int32)
        pool = values_mixed[keep]
        shifts = jnp.concatenate([jnp.full((1,), first, jnp.int32), jnp.full((capacity,), second, jnp.int32), pool[:tiles - 1 - capacity]])
        rest = jax.vmap(lambda inner: jax.random.permutation(inner, tiles - 1))(jax.random.split(keys[2], size)).astype(jnp.int32)
        sends = jnp.concatenate([jnp.zeros((size, 1), jnp.int32), rest + 1], axis=1)
        places = jax.vmap(lambda inner: jax.random.permutation(inner, tiles))(jax.random.split(keys[3], size)).astype(jnp.int32)
        target = jnp.arange(size, dtype=jnp.int32)[:, None]
        source = (target - shifts[None, :]) % size
        local = sends[source, jnp.arange(tiles, dtype=jnp.int32)[None, :]]
        return (jnp.take_along_axis(source, places, 1), jnp.take_along_axis(local, places, 1))
    return jax.vmap(one_group)(jax.random.split(key, groups))


def draw_hilbert_tiles(key, part):
    source, local = tile_order(jax.random.fold_in(key, 11), N_GX, N_GY, TILES_DEV, CAPY, N_GY // 2, N_GY - 1)
    device = jnp.arange(N_GX, dtype=jnp.int32)[:, None, None] * N_GY + source
    return (device * TILES_DEV + local).reshape(-1).astype(jnp.int32)


def draw_morton_tiles(key, part):
    source, local = tile_order(jax.random.fold_in(key, 23), N_GY, N_GX, TILES_DEV, CAPX, N_GX // 2, N_GX - 1)
    device = source * N_GY + jnp.arange(N_GY, dtype=jnp.int32)[:, None, None]
    values = device * TILES_DEV + local
    return jnp.transpose(values, (1, 0, 2)).reshape(-1).astype(jnp.int32)


def saved_input(key, block):
    local_key = jax.random.fold_in(key, 50 + block)
    noise = jax.random.normal(jax.random.fold_in(local_key, 1), (POINTS, C), jnp.float32)
    return jnp.clip(noise, -6.0, 6.0)


def draw_saved_hilbert(key, part):
    return saved_input(key, 0).astype(jnp.bfloat16)


def draw_saved_morton(key, part):
    return saved_input(key, 1).astype(jnp.bfloat16)


def draw_w_qkv(key, part):
    base = jax.random.normal(jax.random.fold_in(key, 61), (BLOCKS, C, 3 * C), jnp.float32) * C ** (-0.5)
    return jnp.clip(base, -4.0, 4.0).astype(jnp.bfloat16)


def levels(key, dims, cuts, smallest, largest):
    level, own = 1.0, jax.random.fold_in(key, 6)
    for dim, shards_of in cuts:
        heights = jnp.exp(jax.random.uniform(jax.random.fold_in(own, dim), (shards_of,), jnp.float32, smallest / len(cuts), largest / len(cuts)))
        level = level * jnp.repeat(heights, dims[dim] // shards_of).reshape([-1 if axis == dim else 1 for axis in range(len(dims))])
    return level


def gaussian(stream_key, dims, spread, bound, cuts=(), kind=jnp.bfloat16):
    drawn = jax.random.normal(stream_key, dims, jnp.float32) * spread
    if len(cuts) > 0:
        drawn = levels(stream_key, dims, cuts, -0.22, 0.18) * drawn
    return jnp.clip(drawn, min=-bound, max=bound).astype(kind)


def setup_inputs(seed: int = 0) -> dict:
    streams_of = jax.random.split(jax.random.key(seed), 9)
    upstream = gaussian(streams_of[0], (POINTS, C), 1.0, 6.0, ((0, 128),))
    saved_hilbert = draw_saved_hilbert(jax.random.fold_in(streams_of[8], 71), 0)
    saved_morton = draw_saved_morton(jax.random.fold_in(streams_of[8], 71), 0)
    gains = jnp.clip(1.0 + 0.18 * jax.random.normal(streams_of[3], (BLOCKS, C), jnp.float32), 0.1, 1.9)
    w_qkv = draw_w_qkv(jax.random.fold_in(streams_of[8], 71), 0)
    w_out = gaussian(streams_of[5], (BLOCKS, C, C), C ** -0.5, 0.375)
    hilbert_tiles = draw_hilbert_tiles(jax.random.fold_in(streams_of[8], 71), 0)
    morton_tiles = draw_morton_tiles(jax.random.fold_in(streams_of[8], 71), 0)
    return dict(upstream=upstream, saved_hilbert=saved_hilbert, saved_morton=saved_morton, gains=gains, w_qkv=w_qkv, w_out=w_out, hilbert_tiles=hilbert_tiles, morton_tiles=morton_tiles)


EPS = 1e-05

def product(form, left, right):
    return jnp.einsum(form, left.astype(jnp.float32), right.astype(jnp.float32))

def norm_parts(inputs, gain):
    values = inputs.astype(jnp.float32)
    row_mean = lax.optimization_barrier(jnp.mean(values, axis=-1, keepdims=True))
    centred = values - row_mean
    inv_scale = lax.rsqrt(lax.optimization_barrier(jnp.mean(centred * centred, axis=-1, keepdims=True)) + EPS)
    normed = centred * inv_scale
    return (normed, inv_scale, (normed * gain).astype(jnp.bfloat16))

def patch_grads(pieces):
    query, keys, values, out_grad = pieces
    group, length, width = query.shape
    head_dim = width // HEADS
    query = query.reshape(group, length, HEADS, head_dim)
    keys = keys.reshape(group, length, HEADS, head_dim)
    values = values.reshape(group, length, HEADS, head_dim)
    out_grad = out_grad.reshape(group, length, HEADS, head_dim)
    scale = head_dim ** (-0.5)
    scores = product('gqhd,gkhd->ghqk', query, keys) * scale
    top = lax.optimization_barrier(jnp.max(scores, axis=-1, keepdims=True))
    weights = jnp.exp(scores - top)
    probs = weights / lax.optimization_barrier(jnp.sum(weights, axis=-1, keepdims=True))
    probs_low = probs.astype(jnp.bfloat16)
    attended = product('ghqk,gkhd->gqhd', probs_low, values).astype(jnp.bfloat16)
    prob_grad = product('gqhd,gkhd->ghqk', out_grad, values)
    value_grad = product('ghqk,gqhd->gkhd', probs_low, out_grad)
    score_grad = (probs * (prob_grad - lax.optimization_barrier(jnp.sum(probs * prob_grad, axis=-1, keepdims=True))) * scale).astype(jnp.bfloat16)
    query_grad = product('ghqk,gkhd->gqhd', score_grad, keys)
    key_grad = product('ghqk,gqhd->gkhd', score_grad, query)
    outputs = (attended, query_grad, key_grad, value_grad)
    return tuple((item.astype(jnp.bfloat16).reshape(group, length, width) for item in outputs))

def block_backward(inputs, grad, gain, w_qkv, w_out):
    rows, width = inputs.shape
    normed, inv_scale, hidden = norm_parts(inputs, gain)
    qkv = jnp.dot(hidden, w_qkv, preferred_element_type=jnp.float32).astype(jnp.bfloat16)
    out_grad = jnp.dot(grad, w_out.T, preferred_element_type=jnp.float32).astype(jnp.bfloat16)
    patches = rows // PATCH
    group = min(2, patches)

    def regroup(array):
        return array.reshape(patches // group, group, PATCH, width)
    pieces = (regroup(qkv[:, :width]), regroup(qkv[:, width:2 * width]), regroup(qkv[:, 2 * width:]), regroup(out_grad))
    results = lax.map(patch_grads, pieces)
    attended, query_grad, key_grad, value_grad = [item.reshape(rows, width) for item in results]
    qkv_grad = jnp.concatenate([query_grad, key_grad, value_grad], axis=1)
    out_weight_grad = jnp.dot(attended.T, grad, preferred_element_type=jnp.float32)
    qkv_weight_grad = jnp.dot(hidden.T, qkv_grad, preferred_element_type=jnp.float32)
    hidden_grad = jnp.dot(qkv_grad, w_qkv.T, preferred_element_type=jnp.float32)
    gain_grad = lax.optimization_barrier(jnp.sum(hidden_grad * normed, axis=0))
    normed_grad = hidden_grad * gain
    correction = normed_grad - lax.optimization_barrier(jnp.mean(normed_grad, axis=-1, keepdims=True)) - normed * lax.optimization_barrier(jnp.mean(normed_grad * normed, axis=-1, keepdims=True))
    input_grad = grad.astype(jnp.float32) + inv_scale * correction
    return (input_grad.astype(jnp.bfloat16), qkv_weight_grad, out_weight_grad, gain_grad)

def reference(upstream, saved_hilbert, saved_morton, gains, w_qkv, w_out, hilbert_tiles, morton_tiles):
    tile_width = TILE * C
    morton_inverse = jnp.argsort(morton_tiles).astype(jnp.int32)
    hilbert_inverse = jnp.argsort(hilbert_tiles).astype(jnp.int32)
    grad_one = upstream.reshape(TILES, tile_width)[morton_tiles].reshape(POINTS, C)
    dx_one, qkv_one, out_one, gain_one = block_backward(saved_morton, grad_one, gains[1], w_qkv[1], w_out[1])
    stored = dx_one.reshape(TILES, tile_width)[morton_inverse]
    grad_zero = stored[hilbert_tiles].reshape(POINTS, C)
    dx_zero, qkv_zero, out_zero, gain_zero = block_backward(saved_hilbert, grad_zero, gains[0], w_qkv[0], w_out[0])
    input_grad = dx_zero.reshape(TILES, tile_width)[hilbert_inverse].reshape(POINTS, C)
    return (input_grad, jnp.stack([qkv_zero, qkv_one]), jnp.stack([out_zero, out_one]), jnp.stack([gain_zero, gain_one]))
```

```python
import jax
import jax.numpy as jnp
from jax import lax
from jax.experimental import pallas as pl
from jax.experimental.pallas import tpu as pltpu
from jax.sharding import PartitionSpec as P

F32 = jnp.float32
BF = jnp.bfloat16
MESH = pl.DeviceIdType.MESH
C = 256
HEADS = 16
HD = 16
TILE = 128
PATCH = 256
EPS = 1e-05
SLAB = 1152
N_GROUPS = 27


def nn(a, b):
    return lax.dot_general(a, b, (((1,), (0,)), ((), ())), preferred_element_type=F32)


def nt(a, b):
    return lax.dot_general(a, b, (((1,), (1,)), ((), ())), preferred_element_type=F32)


def masked(value, head, h):
    return jnp.where(head == h, value, jnp.zeros((), BF))


def forward_norm(x_ref, gain, s):
    rows = x_ref.shape[0]
    for r in range(0, rows, TILE):
        at = slice(r, r + TILE)
        x = x_ref[at, :].astype(F32)
        centred = x - jnp.mean(x, -1, keepdims=True)
        inv = lax.rsqrt(jnp.mean(centred * centred, -1, keepdims=True) + EPS)
        normed = centred * inv
        s["normed"][at, :] = normed
        s["inv"][at, :] = jnp.broadcast_to(inv, (TILE, 128))
        s["hidden"][at, :] = (normed * gain).astype(BF)


def forward_rows(wq_ref, s):
    rows = s["hidden"].shape[0]
    qkv = nn(s["hidden"][...], wq_ref[...]).astype(BF)
    s["q"][...] = qkv[:, :C] * jnp.asarray(0.25, BF)
    s["k"][...] = qkv[:, C : 2 * C]
    s["v"][...] = qkv[:, 2 * C :]
    for p in range(rows // PATCH):
        at = slice(p * PATCH, (p + 1) * PATCH)
        s["qT"][p] = s["q"][at, :].T
        s["kT"][p] = s["k"][at, :].T
        s["vT"][p] = s["v"][at, :].T


def forward_heads(p, s):
    at = slice(p * PATCH, (p + 1) * PATCH)
    head = lax.broadcasted_iota(jnp.int32, (PATCH, C), 1) // HD
    for h in range(HEADS):
        score = nn(masked(s["k"][at, :], head, h), s["qT"][p])
        e = jnp.exp(score - jnp.max(score, axis=0, keepdims=True))
        s["P"][p, h] = (e * (1.0 / jnp.sum(e, axis=0, keepdims=True))).astype(BF)
    for h in range(HEADS):
        at_h = slice(h * HD, (h + 1) * HD)
        s["attT"][p, at_h, :] = nn(s["vT"][p, at_h, :], s["P"][p, h]).astype(BF)


def backward_heads(p, s, w):
    at = slice(p * PATCH, (p + 1) * PATCH)
    head = lax.broadcasted_iota(jnp.int32, (PATCH, C), 1) // HD
    for h in range(HEADS):
        pg = nn(masked(s["v"][at, :], head, h), w["doT"][...])
        pr = s["P"][p, h].astype(F32)
        delta = jnp.sum(pr * pg, axis=0, keepdims=True)
        w["ds"][h] = (pr * (pg - delta)).astype(BF)
    for h in range(HEADS):
        at_h = slice(h * HD, (h + 1) * HD)
        ds = w["ds"][h]
        w["dqT"][at_h, :] = (nn(s["kT"][p, at_h, :], ds) * 0.25).astype(BF)
        w["dkT"][at_h, :] = nt(s["qT"][p, at_h, :], ds).astype(BF)
        w["dvT"][at_h, :] = nt(w["doT"][at_h, :], s["P"][p, h]).astype(BF)


def backward_patch(p, grad_ref, gain, wq_ref, wo_ref, put, s, w):
    at = slice(p * PATCH, (p + 1) * PATCH)
    w["doT"][...] = nt(grad_ref[at, :], wo_ref[...]).astype(BF).T
    backward_heads(p, s, w)
    w["qg"][at, :C] = w["dqT"][...].T
    w["qg"][at, C : 2 * C] = w["dkT"][...].T
    w["qg"][at, 2 * C :] = w["dvT"][...].T
    for t in (2 * p, 2 * p + 1):
        rows = slice(t * TILE, (t + 1) * TILE)
        hg = nt(w["qg"][rows, :], wq_ref[...])
        normed = s["normed"][rows, :]
        gg = jnp.sum(hg * normed, axis=0, keepdims=True)
        if t == 0:
            w["gg"][...] = gg
        else:
            w["gg"][...] += gg
        ng = hg * gain
        mean_ng = jnp.mean(ng, -1, keepdims=True)
        mean_nn = jnp.mean(ng * normed, -1, keepdims=True)
        inv = s["inv"][rows, 0:1]
        put(
            t,
            (
                grad_ref[rows, :].astype(F32) + inv * (ng - mean_ng - normed * mean_nn)
            ).astype(BF),
        )


def weight_grads(grad_ref, s, w, slab):
    slab[1, :, 128:384] = (
        nn(s["attT"][0], grad_ref[:PATCH, :]) + nn(s["attT"][1], grad_ref[PATCH:, :])
    ).astype(BF)
    qkv_part = nn(s["hidden"][...].T, w["qg"][...]).astype(BF)
    slab[0] = qkv_part[:, :640]
    slab[1, :, :128] = qkv_part[:, 640:]
    slab[1, :, 384:512] = jnp.broadcast_to(w["gg"][...], (128, C)).T.astype(BF)
    slab[1, :, 512:] = jnp.zeros((C, 128), BF)


BLOCK_SCRATCH = dict(
    normed=((512, C), F32),
    inv=((512, 128), F32),
    hidden=((512, C), BF),
    q=((512, C), BF),
    k=((512, C), BF),
    v=((512, C), BF),
    qT=((2, C, C), BF),
    kT=((2, C, C), BF),
    vT=((2, C, C), BF),
    P=((2, HEADS, C, C), BF),
    attT=((2, C, C), BF),
)
WORK_SCRATCH = dict(
    doT=((C, C), BF),
    ds=((HEADS, C, C), BF),
    dqT=((C, C), BF),
    dkT=((C, C), BF),
    dvT=((C, C), BF),
    qg=((512, 768), BF),
    gg=((1, C), F32),
)
TILES4 = (4, TILE, C)
LINE = (8, 4, 16, 128)
FAR_GX = ((2, 1), (2, 0), (1, 1), (3, 1), (1, 0), (3, 0), (0, 1))
FAR_GY = sorted(
    ((z, y) for z in range(4) for y in range(4) if (z, y) != (0, 0)),
    key=lambda zy: -sum(min(k, 4 - k) for k in zy),
)
PLANE = (16, 4, 16, 128)
LINE_FLAT = (32, 16, 128)
PLANE_FLAT = (64, 16, 128)
HALF = 640
COMM_SCRATCH = dict(
    a0_hold=(LINE_FLAT, BF),
    a1_hold=(LINE_FLAT, BF),
    a0_pack=(LINE, BF),
    a1_pack=(LINE, BF),
    a0_got=(LINE, BF),
    a1_got=(LINE, BF),
    b0_from=(LINE, BF),
    b1_from=(LINE, BF),
    b0_hold=(LINE_FLAT, BF),
    b1_hold=(LINE_FLAT, BF),
    b0_pack=(LINE, BF),
    b1_pack=(LINE, BF),
    b0_got=(LINE, BF),
    b1_got=(LINE, BF),
    c_from=(PLANE, BF),
    c_hold=(PLANE_FLAT, BF),
    c_pack=(PLANE, BF),
    c_got=(PLANE, BF),
    d_from=(PLANE, BF),
    d_hold=(PLANE_FLAT, BF),
    d_pack=(PLANE, BF),
    d_got=(PLANE, BF),
    grad1=((512, C), BF),
    grad0=((512, C), BF),
    slab1=((2, C, HALF), BF),
    slab0=((2, C, HALF), BF),
    pair1=((C, HALF), BF),
    pair0=((C, HALF), BF),
    both1=((C, HALF), BF),
    both0=((C, HALF), BF),
    red1=((15, 16, HALF), BF),
    red0=((15, 16, HALF), BF),
    redx1=((8, 16, HALF), BF),
    redx0=((8, 16, HALF), BF),
    xm=((512, C), BF),
    xh=((512, C), BF),
    gains=((2, C), F32),
    wq=((2, C, 768), BF),
    wo=((2, C, C), BF),
    tab=((8, 128), jnp.int32),
)


class Links:
    def __init__(self, send_sem, recv_sem):
        self.send_sem, self.recv_sem = send_sem, recv_sem
        self.groups, self.sent = 0, []
        g, gy = lax.axis_index("gx"), lax.axis_index("gy")
        self.g, self.gy = g, gy
        self.core = g % 2
        self.line = [
            lax.rem(g // 2 + x, 4) * 2 + (1 - self.core if c else self.core) for x, c in FAR_GX
        ]
        self.plane = [
            lax.rem(gy // 4 + z, 4) * 4 + lax.rem(gy + y, 4) for z, y in FAR_GY
        ]

    def on_gx(self, g):
        return {"gx": g, "gy": self.gy}

    def on_gy(self, gy):
        return {"gx": self.g, "gy": gy}

    def group(self):
        self.groups += 1
        return self.groups - 1

    def send(self, group, src, dst, device):
        pltpu.make_async_remote_copy(
            src_ref=src,
            dst_ref=dst,
            send_sem=self.send_sem.at[group],
            recv_sem=self.recv_sem.at[group],
            device_id=device,
            device_id_type=MESH,
        ).start()

    def arrived(self, group, ref):
        pltpu.make_async_copy(ref, ref, self.recv_sem.at[group]).wait()
        self.sent.append((group, ref))

    def drain(self):
        for group, ref in self.sent:
            pltpu.make_async_copy(ref, ref, self.send_sem.at[group]).wait()
        self.sent = []

    def greet(self):
        barrier = pltpu.get_barrier_semaphore()
        others = [self.on_gy(gy) for gy in self.plane] + [self.on_gx(g) for g in self.line]
        for other in others:
            pl.semaphore_signal(barrier, inc=1, device_id=other, device_id_type=MESH)

    def greeted(self):
        pl.semaphore_wait(pltpu.get_barrier_semaphore(), 22)


class Exchange:
    def __init__(self, links, others, me, device, source, hold, pack, got, code):
        self.links, self.others, self.me, self.device = links, others, me, device
        self.source, self.hold, self.pack, self.got = source, hold, pack, got
        self.code = code
        self.first, self.second = [], []

    def spread(self, lo, hi):
        part = pl.ds(lo, hi - lo)
        group = self.links.group()
        for i in self.others:
            self.links.send(
                group,
                self.source(i, part),
                self.hold.at[pl.ds(self.me * 4 + lo, hi - lo)],
                self.device(i),
            )
        self.first.append((group, self.hold.at[pl.ds(0, len(self.others) * (hi - lo))]))
        self.keep(lo, hi)

    def keep(self, lo, hi):
        for s in range(lo, hi):
            self.hold[self.me * 4 + s] = self.source(self.me, pl.ds(s, 1))[...].reshape(16, 128)

    def gather(self, lo, hi):
        for group, ref in self.first:
            self.links.arrived(group, ref)
        self.first = []
        part = pl.ds(lo, hi - lo)
        group = self.links.group()
        for r, d in enumerate(self.others):
            for s in range(lo, hi):
                self.pack[r, s] = self.hold[self.code(d, s)]
            self.links.send(
                group, self.pack.at[r, part], self.got.at[self.me, part], self.device(d)
            )
        for s in range(lo, hi):
            self.got[self.me, s] = self.hold[self.code(self.me, s)]
        self.second.append((group, self.got.at[pl.ds(0, len(self.others)), part]))

    def finish(self):
        self.links.arrived(*self.second.pop(0))


class Reduction:
    def __init__(self, links, slab, pair, both, red, redx):
        self.links, self.slab, self.pair, self.both = links, slab, pair, both
        self.red, self.redx = red, redx

    def rows(self, gy):
        return pl.ds(pl.multiple_of(gy * 16, 16), 16)

    def partner(self):
        links = self.links
        self.group = links.group()
        links.send(
            self.group,
            self.slab.at[1 - links.core],
            self.pair,
            links.on_gx(links.g + 1 - 2 * links.core),
        )

    def start(self):
        links = self.links
        links.arrived(self.group, self.pair)
        self.both[...] = (
            self.slab[links.core].astype(F32) + self.pair[...].astype(F32)
        ).astype(BF)
        self.group = links.group()
        for r, to in enumerate(links.plane):
            links.send(
                self.group, self.both.at[self.rows(to)], self.red.at[r], links.on_gy(to)
            )

    def middle(self):
        links = self.links
        links.arrived(self.group, self.red)
        total = self.both[self.rows(links.gy), :].astype(F32)
        for r in range(15):
            total = total + self.red[r].astype(F32)
        self.redx[links.g] = total.astype(BF)
        self.group = links.group()
        for to in links.line:
            links.send(
                self.group, self.redx.at[links.g], self.redx.at[links.g], links.on_gx(to)
            )

    def finish(self):
        self.links.arrived(self.group, self.redx.at[pl.ds(0, 7)])


def kernel(mt_in, ht_in, up, xh_in, xm_in, gains_in, wq_in, wo_in, out_d, out_w, *refs):
    mt, ht, tab_s, send_sem, recv_sem, own_sem = refs[-6:]
    n_b, n_w = len(BLOCK_SCRATCH), len(WORK_SCRATCH)
    s1 = dict(zip(BLOCK_SCRATCH, refs[:n_b]))
    s0 = dict(zip(BLOCK_SCRATCH, refs[n_b : 2 * n_b]))
    w = dict(zip(WORK_SCRATCH, refs[2 * n_b :]))
    m = dict(zip(COMM_SCRATCH, refs[2 * n_b + n_w :]))
    links = Links(send_sem, recv_sem)
    links.greet()
    g, gy = links.g, links.gy
    n_own = [0]

    def bring(src, dst):
        copy = pltpu.make_async_copy(src, dst, own_sem.at[n_own[0]])
        n_own[0] += 1
        copy.start()
        return copy

    wq, wo, gains = m["wq"], m["wo"], m["gains"]
    xm_here = bring(xm_in, m["xm"])
    gains_here = bring(gains_in, gains)
    wq1_here = bring(wq_in.at[1], wq.at[1])
    lists = [bring(mt_in, mt), bring(ht_in, ht)]
    halves = (pl.ds(0, 128), pl.ds(128, 128))
    own_here = [
        bring(up.at[pl.ds(0, 4), g, :, lanes], m[name].at[pl.ds(g * 4, 4)])
        for name, lanes in zip(("a0_hold", "a1_hold"), halves)
    ]
    later = [
        bring(xh_in, m["xh"]),
        bring(wq_in.at[0], wq.at[0]),
        bring(wo_in.at[1], wo.at[1]),
        bring(wo_in.at[0], wo.at[0]),
    ]

    def held_on_line(d, s):
        t = mt[(d * 16 + gy) * 4 + s]
        return ((t >> 6) & 7) * 4 + (t & 3)

    def held_on_plane(d, s):
        return ht[g * 64 + d * 4 + s] & 63

    def back_on_line(d, s):
        return tab_s[0, d * 4 + s] & 31

    def back_on_plane(d, s):
        return tab_s[0, 64 + d * 4 + s] & 63

    def bufs(name):
        return m[name + "_hold"], m[name + "_pack"], m[name + "_got"]

    def line_exchange(name, source, code):
        return Exchange(links, links.line, g, links.on_gx, source, *bufs(name), code)

    a = [
        line_exchange(name, lambda i, p, lanes=lanes: up.at[p, i, :, lanes], held_on_line)
        for name, lanes in zip(("a0", "a1"), halves)
    ]
    b = [
        line_exchange(name, lambda i, p, name=name: m[name + "_from"].at[i, p], back_on_line)
        for name in ("b0", "b1")
    ]
    c = Exchange(
        links, links.plane, gy, links.on_gy, lambda i, p: m["c_from"].at[i, p], *bufs("c"), held_on_plane
    )
    d = Exchange(
        links, links.plane, gy, links.on_gy, lambda i, p: m["d_from"].at[i, p], *bufs("d"), back_on_plane
    )
    red1 = Reduction(links, *(m[n + "1"] for n in ("slab", "pair", "both", "red", "redx")))
    red0 = Reduction(links, *(m[n + "0"] for n in ("slab", "pair", "both", "red", "redx")))

    def put_b(t, tile):
        for i in range(8):
            m["b0_from"][i, t] = tile[16 * i : 16 * i + 16, :128]
            m["b1_from"][i, t] = tile[16 * i : 16 * i + 16, 128:]

    def put_d(t, tile):
        for i in range(16):
            lanes = slice(128 * (i % 2), 128 * (i % 2) + 128)
            m["d_from"][i, t] = tile[16 * (i // 2) : 16 * (i // 2) + 16, lanes]

    def take_a(lo, hi):
        for half in a:
            half.finish()
        for s in range(lo, hi):
            for i in range(8):
                r = s * TILE + 16 * i
                m["grad1"][r : r + 16, :128] = m["a0_got"][i, s]
                m["grad1"][r : r + 16, 128:] = m["a1_got"][i, s]

    def b_to_c(lo, hi):
        for half in b:
            half.finish()
        for s in range(lo, hi):
            for i in range(8):
                m["c_from"][2 * i, s] = m["b0_got"][i, s]
                m["c_from"][2 * i + 1, s] = m["b1_got"][i, s]
        c.spread(lo, hi)

    def take_c(lo, hi):
        c.finish()
        for s in range(lo, hi):
            for i in range(16):
                r = s * TILE + 16 * (i // 2)
                lanes = slice(128 * (i % 2), 128 * (i % 2) + 128)
                m["grad0"][r : r + 16, lanes] = m["c_got"][i, s]

    for half in a:
        half.keep = lambda lo, hi: None
    xm_here.wait()
    gains_here.wait()
    gain0, gain1 = gains[0:1, :], gains[1:2, :]
    forward_norm(m["xm"], gain1, s1)
    links.greeted()
    for half in a:
        half.spread(0, 4)
    wq1_here.wait()
    forward_rows(wq.at[1], s1)
    for copy in lists:
        copy.wait()
    back = jnp.zeros((8, 128), jnp.int32)
    lanes = lax.broadcasted_iota(jnp.int32, (8, 128), 1)
    for j in range(32):
        t = mt[((j // 4) * 16 + gy) * 4 + j % 4]
        back = jnp.where(lanes == ((t >> 6) & 7) * 4 + (t & 3), j, back)
    for j in range(64):
        back = jnp.where(lanes == 64 + (ht[g * 64 + j] & 63), j, back)
    m["tab"][...] = back
    tab_here = bring(m["tab"], tab_s)
    forward_heads(0, s1)
    for copy in own_here:
        copy.wait()
    for lo in (0, 2):
        for half in a:
            half.gather(lo, lo + 2)
    forward_heads(1, s1)
    for copy in later:
        copy.wait()
    forward_norm(m["xh"], gain0, s0)
    forward_rows(wq.at[0], s0)
    forward_heads(0, s0)
    tab_here.wait()

    take_a(0, 2)
    backward_patch(0, m["grad1"], gain1, wq.at[1], wo.at[1], put_b, s1, w)
    for half in b:
        half.spread(0, 2)
    take_a(2, 4)
    backward_patch(1, m["grad1"], gain1, wq.at[1], wo.at[1], put_b, s1, w)
    for half in b:
        half.spread(2, 4)
    weight_grads(m["grad1"], s1, w, m["slab1"])
    for lo in (0, 2):
        for half in b:
            half.gather(lo, lo + 2)
    red1.partner()
    b_to_c(0, 2)
    b_to_c(2, 4)
    forward_heads(1, s0)
    c.gather(0, 2)
    c.gather(2, 4)
    take_c(0, 2)
    red1.start()

    backward_patch(0, m["grad0"], gain0, wq.at[0], wo.at[0], put_d, s0, w)
    d.spread(0, 2)
    take_c(2, 4)
    backward_patch(1, m["grad0"], gain0, wq.at[0], wo.at[0], put_d, s0, w)
    d.spread(2, 4)
    weight_grads(m["grad0"], s0, w, m["slab0"])
    red0.partner()
    red1.middle()
    red0.start()
    d.gather(0, 4)
    red1.finish()
    w1_out = bring(m["redx1"], out_w.at[1])
    d.finish()
    d_out = bring(m["d_got"], out_d)
    red0.middle()
    links.drain()
    red0.finish()
    w0_out = bring(m["redx0"], out_w.at[0])
    links.drain()
    for copy in (w1_out, d_out, w0_out):
        copy.wait()


def write_out(d, sums, out, out_q, out_o, out_g):
    for s in range(4):
        for i in range(16):
            r = s * TILE + 16 * (i // 2)
            lanes = slice(128 * (i % 2), 128 * (i % 2) + 128)
            out[r : r + 16, lanes] = d[i, s]
    diagonal = lax.broadcasted_iota(jnp.int32, (16, 128), 0) == lax.broadcasted_iota(
        jnp.int32, (16, 128), 1
    )
    for b in range(2):
        low, high = (
            sum(sums[b, 2 * x + core].astype(F32) for x in range(4)) for core in (0, 1)
        )
        out_q[b, :, :HALF] = low
        out_q[b, :, HALF:] = high[:, :128]
        out_o[b] = high[:, 128:384]
        row = jnp.sum(jnp.where(diagonal, high[:, 384:512], 0.0), axis=0, keepdims=True)
        out_g[b : b + 1, :] = row[:, :16]


def per_device(up, xh, xm, gains, wq, wo, hilbert_tiles, morton_tiles):
    scratch = (
        list(BLOCK_SCRATCH.values()) * 2
        + list(WORK_SCRATCH.values())
        + list(COMM_SCRATCH.values())
    )
    vmem = pl.BlockSpec(memory_space=pltpu.VMEM)
    hbm = pl.BlockSpec(memory_space=pl.ANY)
    d, sums = pl.pallas_call(
        kernel,
        out_shape=(
            jax.ShapeDtypeStruct(PLANE, BF),
            jax.ShapeDtypeStruct((2, 8, 16, HALF), BF),
        ),
        in_specs=[hbm] * 8,
        out_specs=[hbm] * 2,
        scratch_shapes=[pltpu.VMEM(*v) for v in scratch]
        + [
            pltpu.SMEM((512,), jnp.int32),
            pltpu.SMEM((512,), jnp.int32),
            pltpu.SMEM((8, 128), jnp.int32),
        ]
        + [pltpu.SemaphoreType.DMA((N_GROUPS,))] * 2
        + [pltpu.SemaphoreType.DMA((16,))],
        compiler_params=pltpu.CompilerParams(collective_id=0, has_side_effects=True),
        name="blocks",
    )(morton_tiles, hilbert_tiles, up.reshape(4, 8, 16, C), xh, xm, gains, wq, wo)
    return pl.pallas_call(
        write_out,
        out_shape=(
            jax.ShapeDtypeStruct((512, C), BF),
            jax.ShapeDtypeStruct((2, 16, 768), F32),
            jax.ShapeDtypeStruct((2, 16, 256), F32),
            jax.ShapeDtypeStruct((2, 16), F32),
        ),
        in_specs=[vmem] * 2,
        out_specs=[vmem] * 4,
        name="write_out",
    )(d, sums)


def solution(mesh):
    rows = P(("gx", "gy"), None)
    return jax.shard_map(
        per_device,
        mesh=mesh,
        in_specs=(rows, rows, rows, P(), P(), P(), P(), P()),
        out_specs=(rows, P(None, "gy", None), P(None, "gy", None), P(None, "gy")),
        check_vma=False,
    )
```

```python
import jax
import jax.numpy as jnp
from jax import lax
from jax.experimental import pallas as pl
from jax.experimental.pallas import tpu as pltpu
from jax.sharding import PartitionSpec as P

F32 = jnp.float32
BF = jnp.bfloat16
MESH = pl.DeviceIdType.MESH
C = 256
HEADS = 16
HD = 16
TILE = 128
PATCH = 256
EPS = 1e-05
SLAB = 1152
N_GROUPS = 27


def nn(a, b):
    return lax.dot_general(a, b, (((1,), (0,)), ((), ())), preferred_element_type=F32)


def nt(a, b):
    return lax.dot_general(a, b, (((1,), (1,)), ((), ())), preferred_element_type=F32)


def masked(value, head, h):
    return jnp.where(head == h, value, jnp.zeros((), BF))


def forward_norm(x_ref, gain, s):
    rows = x_ref.shape[0]
    for r in range(0, rows, TILE):
        at = slice(r, r + TILE)
        x = x_ref[at, :].astype(F32)
        centred = x - jnp.mean(x, -1, keepdims=True)
        inv = lax.rsqrt(jnp.mean(centred * centred, -1, keepdims=True) + EPS)
        normed = centred * inv
        s["normed"][at, :] = normed
        s["inv"][at, :] = jnp.broadcast_to(inv, (TILE, 128))
        s["hidden"][at, :] = (normed * gain).astype(BF)


def forward_rows(wq_ref, s):
    rows = s["hidden"].shape[0]
    qkv = nn(s["hidden"][...], wq_ref[...]).astype(BF)
    s["q"][...] = qkv[:, :C] * jnp.asarray(0.25, BF)
    s["k"][...] = qkv[:, C : 2 * C]
    s["v"][...] = qkv[:, 2 * C :]
    for p in range(rows // PATCH):
        at = slice(p * PATCH, (p + 1) * PATCH)
        s["qT"][p] = s["q"][at, :].T
        s["kT"][p] = s["k"][at, :].T
        s["vT"][p] = s["v"][at, :].T


def forward_heads(p, s):
    at = slice(p * PATCH, (p + 1) * PATCH)
    head = lax.broadcasted_iota(jnp.int32, (PATCH, C), 1) // HD
    for h in range(HEADS):
        score = nn(masked(s["k"][at, :], head, h), s["qT"][p])
        e = jnp.exp(score - jnp.max(score, axis=0, keepdims=True))
        s["P"][p, h] = (e * (1.0 / jnp.sum(e, axis=0, keepdims=True))).astype(BF)
    for h in range(HEADS):
        at_h = slice(h * HD, (h + 1) * HD)
        s["attT"][p, at_h, :] = nn(s["vT"][p, at_h, :], s["P"][p, h]).astype(BF)


def backward_heads(p, s, w):
    at = slice(p * PATCH, (p + 1) * PATCH)
    head = lax.broadcasted_iota(jnp.int32, (PATCH, C), 1) // HD
    for h in range(HEADS):
        pg = nn(masked(s["v"][at, :], head, h), w["doT"][...])
        pr = s["P"][p, h].astype(F32)
        delta = jnp.sum(pr * pg, axis=0, keepdims=True)
        w["ds"][h] = (pr * (pg - delta)).astype(BF)
    for h in range(HEADS):
        at_h = slice(h * HD, (h + 1) * HD)
        ds = w["ds"][h]
        w["dqT"][at_h, :] = (nn(s["kT"][p, at_h, :], ds) * 0.25).astype(BF)
        w["dkT"][at_h, :] = nt(s["qT"][p, at_h, :], ds).astype(BF)
        w["dvT"][at_h, :] = nt(w["doT"][at_h, :], s["P"][p, h]).astype(BF)


def backward_patch(p, grad_ref, gain, wq_ref, wo_ref, put, s, w):
    at = slice(p * PATCH, (p + 1) * PATCH)
    w["doT"][...] = nt(grad_ref[at, :], wo_ref[...]).astype(BF).T
    backward_heads(p, s, w)
    w["qg"][at, :C] = w["dqT"][...].T
    w["qg"][at, C : 2 * C] = w["dkT"][...].T
    w["qg"][at, 2 * C :] = w["dvT"][...].T
    for t in (2 * p, 2 * p + 1):
        rows = slice(t * TILE, (t + 1) * TILE)
        hg = nt(w["qg"][rows, :], wq_ref[...])
        normed = s["normed"][rows, :]
        gg = jnp.sum(hg * normed, axis=0, keepdims=True)
        if t == 0:
            w["gg"][...] = gg
        else:
            w["gg"][...] += gg
        ng = hg * gain
        mean_ng = jnp.mean(ng, -1, keepdims=True)
        mean_nn = jnp.mean(ng * normed, -1, keepdims=True)
        inv = s["inv"][rows, 0:1]
        put(
            t,
            (
                grad_ref[rows, :].astype(F32) + inv * (ng - mean_ng - normed * mean_nn)
            ).astype(BF),
        )


def weight_grads(grad_ref, s, w, slab):
    slab[1, :, 128:384] = (
        nn(s["attT"][0], grad_ref[:PATCH, :]) + nn(s["attT"][1], grad_ref[PATCH:, :])
    ).astype(BF)
    qkv_part = nn(s["hidden"][...].T, w["qg"][...]).astype(BF)
    slab[0] = qkv_part[:, :640]
    slab[1, :, :128] = qkv_part[:, 640:]
    slab[1, :, 384:512] = jnp.broadcast_to(w["gg"][...], (128, C)).T.astype(BF)
    slab[1, :, 512:] = jnp.zeros((C, 128), BF)


BLOCK_SCRATCH = dict(
    normed=((512, C), F32),
    inv=((512, 128), F32),
    hidden=((512, C), BF),
    q=((512, C), BF),
    k=((512, C), BF),
    v=((512, C), BF),
    qT=((2, C, C), BF),
    kT=((2, C, C), BF),
    vT=((2, C, C), BF),
    P=((2, HEADS, C, C), BF),
    attT=((2, C, C), BF),
)
WORK_SCRATCH = dict(
    doT=((C, C), BF),
    ds=((HEADS, C, C), BF),
    dqT=((C, C), BF),
    dkT=((C, C), BF),
    dvT=((C, C), BF),
    qg=((512, 768), BF),
    gg=((1, C), F32),
)
TILES4 = (4, TILE, C)
LINE = (8, 4, 16, 128)
FAR_GX = ((2, 1), (2, 0), (1, 1), (3, 1), (1, 0), (3, 0), (0, 1))
FAR_GY = sorted(
    ((z, y) for z in range(4) for y in range(4) if (z, y) != (0, 0)),
    key=lambda zy: -sum(min(k, 4 - k) for k in zy),
)
PLANE = (16, 4, 16, 128)
LINE_FLAT = (32, 16, 128)
PLANE_FLAT = (64, 16, 128)
HALF = 640
COMM_SCRATCH = dict(
    a0_hold=(LINE_FLAT, BF),
    a1_hold=(LINE_FLAT, BF),
    a0_pack=(LINE, BF),
    a1_pack=(LINE, BF),
    a0_got=(LINE, BF),
    a1_got=(LINE, BF),
    b0_from=(LINE, BF),
    b1_from=(LINE, BF),
    b0_hold=(LINE_FLAT, BF),
    b1_hold=(LINE_FLAT, BF),
    b0_pack=(LINE, BF),
    b1_pack=(LINE, BF),
    b0_got=(LINE, BF),
    b1_got=(LINE, BF),
    c_from=(PLANE, BF),
    c_hold=(PLANE_FLAT, BF),
    c_pack=(PLANE, BF),
    c_got=(PLANE, BF),
    d_from=(PLANE, BF),
    d_hold=(PLANE_FLAT, BF),
    d_pack=(PLANE, BF),
    d_got=(PLANE, BF),
    grad1=((512, C), BF),
    grad0=((512, C), BF),
    slab1=((2, C, HALF), BF),
    slab0=((2, C, HALF), BF),
    pair1=((C, HALF), BF),
    pair0=((C, HALF), BF),
    both1=((C, HALF), BF),
    both0=((C, HALF), BF),
    red1=((15, 16, HALF), BF),
    red0=((15, 16, HALF), BF),
    redx1=((8, 16, HALF), BF),
    redx0=((8, 16, HALF), BF),
    xm=((512, C), BF),
    xh=((512, C), BF),
    gains=((2, C), F32),
    wq=((2, C, 768), BF),
    wo=((2, C, C), BF),
    tab=((8, 128), jnp.int32),
)


class Links:
    def __init__(self, send_sem, recv_sem):
        self.send_sem, self.recv_sem = send_sem, recv_sem
        self.groups, self.sent = 0, []
        g, gy = lax.axis_index("gx"), lax.axis_index("gy")
        self.g, self.gy = g, gy
        self.core = g % 2
        self.line = [
            lax.rem(g // 2 + x, 4) * 2 + (1 - self.core if c else self.core) for x, c in FAR_GX
        ]
        self.plane = [
            lax.rem(gy // 4 + z, 4) * 4 + lax.rem(gy + y, 4) for z, y in FAR_GY
        ]

    def on_gx(self, g):
        return {"gx": g, "gy": self.gy}

    def on_gy(self, gy):
        return {"gx": self.g, "gy": gy}

    def group(self):
        self.groups += 1
        return self.groups - 1

    def send(self, group, src, dst, device):
        pltpu.make_async_remote_copy(
            src_ref=src,
            dst_ref=dst,
            send_sem=self.send_sem.at[group],
            recv_sem=self.recv_sem.at[group],
            device_id=device,
            device_id_type=MESH,
        ).start()

    def arrived(self, group, ref):
        pltpu.make_async_copy(ref, ref, self.recv_sem.at[group]).wait()
        self.sent.append((group, ref))

    def drain(self):
        for group, ref in self.sent:
            pltpu.make_async_copy(ref, ref, self.send_sem.at[group]).wait()
        self.sent = []

    def greet(self):
        barrier = pltpu.get_barrier_semaphore()
        others = [self.on_gy(gy) for gy in self.plane] + [self.on_gx(g) for g in self.line]
        for other in others:
            pl.semaphore_signal(barrier, inc=1, device_id=other, device_id_type=MESH)

    def greeted(self):
        pl.semaphore_wait(pltpu.get_barrier_semaphore(), 22)


class Exchange:
    def __init__(self, links, others, me, device, source, hold, pack, got, code):
        self.links, self.others, self.me, self.device = links, others, me, device
        self.source, self.hold, self.pack, self.got = source, hold, pack, got
        self.code = code
        self.first, self.second = [], []

    def spread(self, lo, hi):
        part = pl.ds(lo, hi - lo)
        group = self.links.group()
        for i in self.others:
            self.links.send(
                group,
                self.source(i, part),
                self.hold.at[pl.ds(self.me * 4 + lo, hi - lo)],
                self.device(i),
            )
        self.first.append((group, self.hold.at[pl.ds(0, len(self.others) * (hi - lo))]))
        self.keep(lo, hi)

    def keep(self, lo, hi):
        for s in range(lo, hi):
            self.hold[self.me * 4 + s] = self.source(self.me, pl.ds(s, 1))[...].reshape(16, 128)

    def gather(self, lo, hi):
        for group, ref in self.first:
            self.links.arrived(group, ref)
        self.first = []
        part = pl.ds(lo, hi - lo)
        group = self.links.group()
        for r, d in enumerate(self.others):
            for s in range(lo, hi):
                self.pack[r, s] = self.hold[self.code(d, s)]
            self.links.send(
                group, self.pack.at[r, part], self.got.at[self.me, part], self.device(d)
            )
        for s in range(lo, hi):
            self.got[self.me, s] = self.hold[self.code(self.me, s)]
        self.second.append((group, self.got.at[pl.ds(0, len(self.others)), part]))

    def finish(self):
        self.links.arrived(*self.second.pop(0))


class Reduction:
    def __init__(self, links, slab, pair, both, red, redx):
        self.links, self.slab, self.pair, self.both = links, slab, pair, both
        self.red, self.redx = red, redx

    def rows(self, gy):
        return pl.ds(pl.multiple_of(gy * 16, 16), 16)

    def partner(self):
        links = self.links
        self.group = links.group()
        links.send(
            self.group,
            self.slab.at[1 - links.core],
            self.pair,
            links.on_gx(links.g + 1 - 2 * links.core),
        )

    def start(self):
        links = self.links
        links.arrived(self.group, self.pair)
        self.both[...] = (
            self.slab[links.core].astype(F32) + self.pair[...].astype(F32)
        ).astype(BF)
        self.group = links.group()
        for r, to in enumerate(links.plane):
            links.send(
                self.group, self.both.at[self.rows(to)], self.red.at[r], links.on_gy(to)
            )

    def middle(self):
        links = self.links
        links.arrived(self.group, self.red)
        total = self.both[self.rows(links.gy), :].astype(F32)
        for r in range(15):
            total = total + self.red[r].astype(F32)
        self.redx[links.g] = total.astype(BF)
        self.group = links.group()
        for to in links.line:
            links.send(
                self.group, self.redx.at[links.g], self.redx.at[links.g], links.on_gx(to)
            )

    def finish(self):
        self.links.arrived(self.group, self.redx.at[pl.ds(0, 7)])


def kernel(mt_in, ht_in, up, xh_in, xm_in, gains_in, wq_in, wo_in, out_d, out_w, *refs):
    mt, ht, tab_s, send_sem, recv_sem, own_sem = refs[-6:]
    n_b, n_w = len(BLOCK_SCRATCH), len(WORK_SCRATCH)
    s1 = dict(zip(BLOCK_SCRATCH, refs[:n_b]))
    s0 = dict(zip(BLOCK_SCRATCH, refs[n_b : 2 * n_b]))
    w = dict(zip(WORK_SCRATCH, refs[2 * n_b :]))
    m = dict(zip(COMM_SCRATCH, refs[2 * n_b + n_w :]))
    links = Links(send_sem, recv_sem)
    links.greet()
    g, gy = links.g, links.gy
    n_own = [0]

    def bring(src, dst):
        copy = pltpu.make_async_copy(src, dst, own_sem.at[n_own[0]])
        n_own[0] += 1
        copy.start()
        return copy

    wq, wo, gains = m["wq"], m["wo"], m["gains"]
    xm_here = bring(xm_in, m["xm"])
    gains_here = bring(gains_in, gains)
    wq1_here = bring(wq_in.at[1], wq.at[1])
    lists = [bring(mt_in, mt), bring(ht_in, ht)]
    halves = (pl.ds(0, 128), pl.ds(128, 128))
    own_here = [
        bring(up.at[pl.ds(0, 4), g, :, lanes], m[name].at[pl.ds(g * 4, 4)])
        for name, lanes in zip(("a0_hold", "a1_hold"), halves)
    ]
    later = [
        bring(xh_in, m["xh"]),
        bring(wq_in.at[0], wq.at[0]),
        bring(wo_in.at[1], wo.at[1]),
        bring(wo_in.at[0], wo.at[0]),
    ]

    def held_on_line(d, s):
        t = mt[(d * 16 + gy) * 4 + s]
        return ((t >> 6) & 7) * 4 + (t & 3)

    def held_on_plane(d, s):
        return ht[g * 64 + d * 4 + s] & 63

    def back_on_line(d, s):
        return tab_s[0, d * 4 + s] & 31

    def back_on_plane(d, s):
        return tab_s[0, 64 + d * 4 + s] & 63

    def bufs(name):
        return m[name + "_hold"], m[name + "_pack"], m[name + "_got"]

    def line_exchange(name, source, code):
        return Exchange(links, links.line, g, links.on_gx, source, *bufs(name), code)

    a = [
        line_exchange(name, lambda i, p, lanes=lanes: up.at[p, i, :, lanes], held_on_line)
        for name, lanes in zip(("a0", "a1"), halves)
    ]
    b = [
        line_exchange(name, lambda i, p, name=name: m[name + "_from"].at[i, p], back_on_line)
        for name in ("b0", "b1")
    ]
    c = Exchange(
        links, links.plane, gy, links.on_gy, lambda i, p: m["c_from"].at[i, p], *bufs("c"), held_on_plane
    )
    d = Exchange(
        links, links.plane, gy, links.on_gy, lambda i, p: m["d_from"].at[i, p], *bufs("d"), back_on_plane
    )
    red1 = Reduction(links, *(m[n + "1"] for n in ("slab", "pair", "both", "red", "redx")))
    red0 = Reduction(links, *(m[n + "0"] for n in ("slab", "pair", "both", "red", "redx")))

    def put_b(t, tile):
        for i in range(8):
            m["b0_from"][i, t] = tile[16 * i : 16 * i + 16, :128]
            m["b1_from"][i, t] = tile[16 * i : 16 * i + 16, 128:]

    def put_d(t, tile):
        for i in range(16):
            lanes = slice(128 * (i % 2), 128 * (i % 2) + 128)
            m["d_from"][i, t] = tile[16 * (i // 2) : 16 * (i // 2) + 16, lanes]

    def take_a(lo, hi):
        for half in a:
            half.finish()
        for s in range(lo, hi):
            for i in range(8):
                r = s * TILE + 16 * i
                m["grad1"][r : r + 16, :128] = m["a0_got"][i, s]
                m["grad1"][r : r + 16, 128:] = m["a1_got"][i, s]

    def b_to_c(lo, hi):
        for half in b:
            half.finish()
        for s in range(lo, hi):
            for i in range(8):
                m["c_from"][2 * i, s] = m["b0_got"][i, s]
                m["c_from"][2 * i + 1, s] = m["b1_got"][i, s]
        c.spread(lo, hi)

    def take_c(lo, hi):
        c.finish()
        for s in range(lo, hi):
            for i in range(16):
                r = s * TILE + 16 * (i // 2)
                lanes = slice(128 * (i % 2), 128 * (i % 2) + 128)
                m["grad0"][r : r + 16, lanes] = m["c_got"][i, s]

    def apart(*work):
        @pl.when(g >= 0)
        def _():
            for piece in work:
                piece()

    for half in a:
        half.keep = lambda lo, hi: None
    xm_here.wait()
    gains_here.wait()
    gain0, gain1 = gains[0:1, :], gains[1:2, :]
    forward_norm(m["xm"], gain1, s1)
    links.greeted()
    for half in a:
        half.spread(0, 4)
    wq1_here.wait()
    forward_rows(wq.at[1], s1)
    for copy in lists:
        copy.wait()
    back = jnp.zeros((8, 128), jnp.int32)
    lanes = lax.broadcasted_iota(jnp.int32, (8, 128), 1)
    for j in range(32):
        t = mt[((j // 4) * 16 + gy) * 4 + j % 4]
        back = jnp.where(lanes == ((t >> 6) & 7) * 4 + (t & 3), j, back)
    for j in range(64):
        back = jnp.where(lanes == 64 + (ht[g * 64 + j] & 63), j, back)
    m["tab"][...] = back
    tab_here = bring(m["tab"], tab_s)
    apart(lambda: forward_heads(0, s1), lambda: forward_heads(1, s1))
    for copy in own_here:
        copy.wait()
    for lo in (0, 2):
        for half in a:
            half.gather(lo, lo + 2)
    for copy in later:
        copy.wait()
    apart(
        lambda: forward_norm(m["xh"], gain0, s0),
        lambda: forward_rows(wq.at[0], s0),
        lambda: forward_heads(0, s0),
        lambda: forward_heads(1, s0),
    )
    tab_here.wait()

    take_a(0, 2)
    backward_patch(0, m["grad1"], gain1, wq.at[1], wo.at[1], put_b, s1, w)
    for half in b:
        half.spread(0, 2)
    take_a(2, 4)
    backward_patch(1, m["grad1"], gain1, wq.at[1], wo.at[1], put_b, s1, w)
    for half in b:
        half.spread(2, 4)
    weight_grads(m["grad1"], s1, w, m["slab1"])
    for lo in (0, 2):
        for half in b:
            half.gather(lo, lo + 2)
    red1.partner()
    b_to_c(0, 2)
    b_to_c(2, 4)
    c.gather(0, 2)
    c.gather(2, 4)
    take_c(0, 2)
    red1.start()

    backward_patch(0, m["grad0"], gain0, wq.at[0], wo.at[0], put_d, s0, w)
    d.spread(0, 2)
    take_c(2, 4)
    backward_patch(1, m["grad0"], gain0, wq.at[0], wo.at[0], put_d, s0, w)
    d.spread(2, 4)
    weight_grads(m["grad0"], s0, w, m["slab0"])
    red0.partner()
    red1.middle()
    red0.start()
    d.gather(0, 4)
    red1.finish()
    w1_out = bring(m["redx1"], out_w.at[1])
    d.finish()
    d_out = bring(m["d_got"], out_d)
    red0.middle()
    links.drain()
    red0.finish()
    w0_out = bring(m["redx0"], out_w.at[0])
    links.drain()
    for copy in (w1_out, d_out, w0_out):
        copy.wait()


def write_out(d, sums, out, out_q, out_o, out_g):
    for s in range(4):
        for i in range(16):
            r = s * TILE + 16 * (i // 2)
            lanes = slice(128 * (i % 2), 128 * (i % 2) + 128)
            out[r : r + 16, lanes] = d[i, s]
    diagonal = lax.broadcasted_iota(jnp.int32, (16, 128), 0) == lax.broadcasted_iota(
        jnp.int32, (16, 128), 1
    )
    for b in range(2):
        low, high = (
            sum(sums[b, 2 * x + core].astype(F32) for x in range(4)) for core in (0, 1)
        )
        out_q[b, :, :HALF] = low
        out_q[b, :, HALF:] = high[:, :128]
        out_o[b] = high[:, 128:384]
        row = jnp.sum(jnp.where(diagonal, high[:, 384:512], 0.0), axis=0, keepdims=True)
        out_g[b : b + 1, :] = row[:, :16]


def per_device(up, xh, xm, gains, wq, wo, hilbert_tiles, morton_tiles):
    scratch = (
        list(BLOCK_SCRATCH.values()) * 2
        + list(WORK_SCRATCH.values())
        + list(COMM_SCRATCH.values())
    )
    vmem = pl.BlockSpec(memory_space=pltpu.VMEM)
    hbm = pl.BlockSpec(memory_space=pl.ANY)
    d, sums = pl.pallas_call(
        kernel,
        out_shape=(
            jax.ShapeDtypeStruct(PLANE, BF),
            jax.ShapeDtypeStruct((2, 8, 16, HALF), BF),
        ),
        in_specs=[hbm] * 8,
        out_specs=[hbm] * 2,
        scratch_shapes=[pltpu.VMEM(*v) for v in scratch]
        + [
            pltpu.SMEM((512,), jnp.int32),
            pltpu.SMEM((512,), jnp.int32),
            pltpu.SMEM((8, 128), jnp.int32),
        ]
        + [pltpu.SemaphoreType.DMA((N_GROUPS,))] * 2
        + [pltpu.SemaphoreType.DMA((16,))],
        compiler_params=pltpu.CompilerParams(collective_id=0, has_side_effects=True),
        name="blocks",
    )(morton_tiles, hilbert_tiles, up.reshape(4, 8, 16, C), xh, xm, gains, wq, wo)
    return pl.pallas_call(
        write_out,
        out_shape=(
            jax.ShapeDtypeStruct((512, C), BF),
            jax.ShapeDtypeStruct((2, 16, 768), F32),
            jax.ShapeDtypeStruct((2, 16, 256), F32),
            jax.ShapeDtypeStruct((2, 16), F32),
        ),
        in_specs=[vmem] * 2,
        out_specs=[vmem] * 4,
        name="write_out",
    )(d, sums)


def solution(mesh):
    rows = P(("gx", "gy"), None)
    return jax.shard_map(
        per_device,
        mesh=mesh,
        in_specs=(rows, rows, rows, P(), P(), P(), P(), P()),
        out_specs=(rows, P(None, "gy", None), P(None, "gy", None), P(None, "gy")),
        check_vma=False,
    )
```

```python
import jax
import jax.numpy as jnp
from jax import lax
from jax.experimental import pallas as pl
from jax.experimental.pallas import tpu as pltpu
from jax.sharding import PartitionSpec as P

F32 = jnp.float32
BF = jnp.bfloat16
MESH = pl.DeviceIdType.MESH
C = 256
HEADS = 16
HD = 16
TILE = 128
PATCH = 256
EPS = 1e-05
SLAB = 1152
N_GROUPS = 27


def nn(a, b):
    return lax.dot_general(a, b, (((1,), (0,)), ((), ())), preferred_element_type=F32)


def nt(a, b):
    return lax.dot_general(a, b, (((1,), (1,)), ((), ())), preferred_element_type=F32)


def masked(value, head, h):
    return jnp.where(head == h, value, jnp.zeros((), BF))


def forward_norm(x_ref, gain, s):
    rows = x_ref.shape[0]
    for r in range(0, rows, TILE):
        at = slice(r, r + TILE)
        x = x_ref[at, :].astype(F32)
        centred = x - jnp.mean(x, -1, keepdims=True)
        inv = lax.rsqrt(jnp.mean(centred * centred, -1, keepdims=True) + EPS)
        normed = centred * inv
        s["normed"][at, :] = normed
        s["inv"][at, :] = jnp.broadcast_to(inv, (TILE, 128))
        s["hidden"][at, :] = (normed * gain).astype(BF)


def forward_rows(wq_ref, s):
    rows = s["hidden"].shape[0]
    qkv = nn(s["hidden"][...], wq_ref[...]).astype(BF)
    s["q"][...] = qkv[:, :C] * jnp.asarray(0.25, BF)
    s["k"][...] = qkv[:, C : 2 * C]
    s["v"][...] = qkv[:, 2 * C :]
    for p in range(rows // PATCH):
        at = slice(p * PATCH, (p + 1) * PATCH)
        s["qT"][p] = s["q"][at, :].T
        s["kT"][p] = s["k"][at, :].T
        s["vT"][p] = s["v"][at, :].T


def forward_heads(p, s):
    at = slice(p * PATCH, (p + 1) * PATCH)
    head = lax.broadcasted_iota(jnp.int32, (PATCH, C), 1) // HD
    for h in range(HEADS):
        score = nn(masked(s["k"][at, :], head, h), s["qT"][p])
        e = jnp.exp(score - jnp.max(score, axis=0, keepdims=True))
        s["P"][p, h] = (e * (1.0 / jnp.sum(e, axis=0, keepdims=True))).astype(BF)
    for h in range(HEADS):
        at_h = slice(h * HD, (h + 1) * HD)
        s["attT"][p, at_h, :] = nn(s["vT"][p, at_h, :], s["P"][p, h]).astype(BF)


def backward_heads(p, s, w):
    at = slice(p * PATCH, (p + 1) * PATCH)
    head = lax.broadcasted_iota(jnp.int32, (PATCH, C), 1) // HD
    for h in range(HEADS):
        pg = nn(masked(s["v"][at, :], head, h), w["doT"][...])
        pr = s["P"][p, h].astype(F32)
        delta = jnp.sum(pr * pg, axis=0, keepdims=True)
        w["ds"][h] = (pr * (pg - delta)).astype(BF)
    for h in range(HEADS):
        at_h = slice(h * HD, (h + 1) * HD)
        ds = w["ds"][h]
        w["dqT"][at_h, :] = (nn(s["kT"][p, at_h, :], ds) * 0.25).astype(BF)
        w["dkT"][at_h, :] = nt(s["qT"][p, at_h, :], ds).astype(BF)
        w["dvT"][at_h, :] = nt(w["doT"][at_h, :], s["P"][p, h]).astype(BF)


def backward_patch(p, grad_ref, gain, wq_ref, wo_ref, put, s, w):
    at = slice(p * PATCH, (p + 1) * PATCH)
    w["doT"][...] = nt(grad_ref[at, :], wo_ref[...]).astype(BF).T
    backward_heads(p, s, w)
    w["qg"][at, :C] = w["dqT"][...].T
    w["qg"][at, C : 2 * C] = w["dkT"][...].T
    w["qg"][at, 2 * C :] = w["dvT"][...].T
    for t in (2 * p, 2 * p + 1):
        rows = slice(t * TILE, (t + 1) * TILE)
        hg = nt(w["qg"][rows, :], wq_ref[...])
        normed = s["normed"][rows, :]
        gg = jnp.sum(hg * normed, axis=0, keepdims=True)
        if t == 0:
            w["gg"][...] = gg
        else:
            w["gg"][...] += gg
        ng = hg * gain
        mean_ng = jnp.mean(ng, -1, keepdims=True)
        mean_nn = jnp.mean(ng * normed, -1, keepdims=True)
        inv = s["inv"][rows, 0:1]
        put(
            t,
            (
                grad_ref[rows, :].astype(F32) + inv * (ng - mean_ng - normed * mean_nn)
            ).astype(BF),
        )


def weight_grads(grad_ref, s, w, slab):
    slab[1, :, 128:384] = (
        nn(s["attT"][0], grad_ref[:PATCH, :]) + nn(s["attT"][1], grad_ref[PATCH:, :])
    ).astype(BF)
    qkv_part = nn(s["hidden"][...].T, w["qg"][...]).astype(BF)
    slab[0] = qkv_part[:, :640]
    slab[1, :, :128] = qkv_part[:, 640:]
    slab[1, :, 384:512] = jnp.broadcast_to(w["gg"][...], (128, C)).T.astype(BF)
    slab[1, :, 512:] = jnp.zeros((C, 128), BF)


BLOCK_SCRATCH = dict(
    normed=((512, C), F32),
    inv=((512, 128), F32),
    hidden=((512, C), BF),
    q=((512, C), BF),
    k=((512, C), BF),
    v=((512, C), BF),
    qT=((2, C, C), BF),
    kT=((2, C, C), BF),
    vT=((2, C, C), BF),
    P=((2, HEADS, C, C), BF),
    attT=((2, C, C), BF),
)
WORK_SCRATCH = dict(
    doT=((C, C), BF),
    ds=((HEADS, C, C), BF),
    dqT=((C, C), BF),
    dkT=((C, C), BF),
    dvT=((C, C), BF),
    qg=((512, 768), BF),
    gg=((1, C), F32),
)
TILES4 = (4, TILE, C)
LINE = (8, 4, 16, 128)
FAR_GX = ((2, 1), (2, 0), (1, 1), (3, 1), (1, 0), (3, 0), (0, 1))
FAR_GY = sorted(
    ((z, y) for z in range(4) for y in range(4) if (z, y) != (0, 0)),
    key=lambda zy: -sum(min(k, 4 - k) for k in zy),
)
PLANE = (16, 4, 16, 128)
LINE_FLAT = (32, 16, 128)
PLANE_FLAT = (64, 16, 128)
HALF = 640
COMM_SCRATCH = dict(
    a0_hold=(LINE_FLAT, BF),
    a1_hold=(LINE_FLAT, BF),
    a0_pack=(LINE, BF),
    a1_pack=(LINE, BF),
    a0_got=(LINE, BF),
    a1_got=(LINE, BF),
    b0_from=(LINE, BF),
    b1_from=(LINE, BF),
    b0_hold=(LINE_FLAT, BF),
    b1_hold=(LINE_FLAT, BF),
    b0_pack=(LINE, BF),
    b1_pack=(LINE, BF),
    b0_got=(LINE, BF),
    b1_got=(LINE, BF),
    c_from=(PLANE, BF),
    c_hold=(PLANE_FLAT, BF),
    c_pack=(PLANE, BF),
    c_got=(PLANE, BF),
    d_from=(PLANE, BF),
    d_hold=(PLANE_FLAT, BF),
    d_pack=(PLANE, BF),
    d_got=(PLANE, BF),
    grad1=((512, C), BF),
    grad0=((512, C), BF),
    slab1=((2, C, HALF), BF),
    slab0=((2, C, HALF), BF),
    pair1=((C, HALF), BF),
    pair0=((C, HALF), BF),
    both1=((C, HALF), BF),
    both0=((C, HALF), BF),
    red1=((15, 16, HALF), BF),
    red0=((15, 16, HALF), BF),
    redx1=((8, 16, HALF), BF),
    redx0=((8, 16, HALF), BF),
    xm=((512, C), BF),
    xh=((512, C), BF),
    gains=((2, C), F32),
    wq=((2, C, 768), BF),
    wo=((2, C, C), BF),
    tab=((8, 128), jnp.int32),
)


class Links:
    def __init__(self, send_sem, recv_sem):
        self.send_sem, self.recv_sem = send_sem, recv_sem
        self.groups, self.sent = 0, []
        g, gy = lax.axis_index("gx"), lax.axis_index("gy")
        self.g, self.gy = g, gy
        self.core = g % 2
        self.line = [
            lax.rem(g // 2 + x, 4) * 2 + (1 - self.core if c else self.core) for x, c in FAR_GX
        ]
        self.plane = [
            lax.rem(gy // 4 + z, 4) * 4 + lax.rem(gy + y, 4) for z, y in FAR_GY
        ]

    def on_gx(self, g):
        return {"gx": g, "gy": self.gy}

    def on_gy(self, gy):
        return {"gx": self.g, "gy": gy}

    def group(self):
        self.groups += 1
        return self.groups - 1

    def send(self, group, src, dst, device):
        pltpu.make_async_remote_copy(
            src_ref=src,
            dst_ref=dst,
            send_sem=self.send_sem.at[group],
            recv_sem=self.recv_sem.at[group],
            device_id=device,
            device_id_type=MESH,
        ).start()

    def arrived(self, group, ref):
        pltpu.make_async_copy(ref, ref, self.recv_sem.at[group]).wait()
        self.sent.append((group, ref))

    def drain(self):
        for group, ref in self.sent:
            pltpu.make_async_copy(ref, ref, self.send_sem.at[group]).wait()
        self.sent = []

    def greet(self):
        barrier = pltpu.get_barrier_semaphore()
        others = [self.on_gy(gy) for gy in self.plane] + [self.on_gx(g) for g in self.line]
        for other in others:
            pl.semaphore_signal(barrier, inc=1, device_id=other, device_id_type=MESH)

    def greeted(self):
        pl.semaphore_wait(pltpu.get_barrier_semaphore(), 22)


class Exchange:
    def __init__(self, links, others, me, device, source, hold, pack, got, code):
        self.links, self.others, self.me, self.device = links, others, me, device
        self.source, self.hold, self.pack, self.got = source, hold, pack, got
        self.code = code
        self.first, self.second = [], []

    def spread(self, lo, hi):
        part = pl.ds(lo, hi - lo)
        group = self.links.group()
        for i in self.others:
            self.links.send(
                group,
                self.source(i, part),
                self.hold.at[pl.ds(self.me * 4 + lo, hi - lo)],
                self.device(i),
            )
        self.first.append((group, self.hold.at[pl.ds(0, len(self.others) * (hi - lo))]))
        self.keep(lo, hi)

    def keep(self, lo, hi):
        for s in range(lo, hi):
            self.hold[self.me * 4 + s] = self.source(self.me, pl.ds(s, 1))[...].reshape(16, 128)

    def gather(self, lo, hi):
        for group, ref in self.first:
            self.links.arrived(group, ref)
        self.first = []
        part = pl.ds(lo, hi - lo)
        group = self.links.group()
        for r, d in enumerate(self.others):
            for s in range(lo, hi):
                self.pack[r, s] = self.hold[self.code(d, s)]
            self.links.send(
                group, self.pack.at[r, part], self.got.at[self.me, part], self.device(d)
            )
        for s in range(lo, hi):
            self.got[self.me, s] = self.hold[self.code(self.me, s)]
        self.second.append((group, self.got.at[pl.ds(0, len(self.others)), part]))

    def finish(self):
        self.links.arrived(*self.second.pop(0))


class Reduction:
    def __init__(self, links, slab, pair, both, red, redx):
        self.links, self.slab, self.pair, self.both = links, slab, pair, both
        self.red, self.redx = red, redx

    def rows(self, gy):
        return pl.ds(pl.multiple_of(gy * 16, 16), 16)

    def partner(self):
        links = self.links
        self.group = links.group()
        links.send(
            self.group,
            self.slab.at[1 - links.core],
            self.pair,
            links.on_gx(links.g + 1 - 2 * links.core),
        )

    def start(self):
        links = self.links
        links.arrived(self.group, self.pair)
        self.both[...] = (
            self.slab[links.core].astype(F32) + self.pair[...].astype(F32)
        ).astype(BF)
        self.group = links.group()
        for r, to in enumerate(links.plane):
            links.send(
                self.group, self.both.at[self.rows(to)], self.red.at[r], links.on_gy(to)
            )

    def middle(self):
        links = self.links
        links.arrived(self.group, self.red)
        total = self.both[self.rows(links.gy), :].astype(F32)
        for r in range(15):
            total = total + self.red[r].astype(F32)
        self.redx[links.g] = total.astype(BF)
        self.group = links.group()
        for to in links.line:
            links.send(
                self.group, self.redx.at[links.g], self.redx.at[links.g], links.on_gx(to)
            )

    def finish(self):
        self.links.arrived(self.group, self.redx.at[pl.ds(0, 7)])


def kernel(mt_in, ht_in, up, xh_in, xm_in, gains_in, wq_in, wo_in, out_d, out_w, *refs):
    mt, ht, tab_s, send_sem, recv_sem, own_sem = refs[-6:]
    n_b, n_w = len(BLOCK_SCRATCH), len(WORK_SCRATCH)
    s1 = dict(zip(BLOCK_SCRATCH, refs[:n_b]))
    s0 = dict(zip(BLOCK_SCRATCH, refs[n_b : 2 * n_b]))
    w = dict(zip(WORK_SCRATCH, refs[2 * n_b :]))
    m = dict(zip(COMM_SCRATCH, refs[2 * n_b + n_w :]))
    links = Links(send_sem, recv_sem)
    links.greet()
    g, gy = links.g, links.gy
    n_own = [0]

    def bring(src, dst):
        copy = pltpu.make_async_copy(src, dst, own_sem.at[n_own[0]])
        n_own[0] += 1
        copy.start()
        return copy

    wq, wo, gains = m["wq"], m["wo"], m["gains"]
    xm_here = bring(xm_in, m["xm"])
    gains_here = bring(gains_in, gains)
    wq1_here = bring(wq_in.at[1], wq.at[1])
    lists = [bring(mt_in, mt), bring(ht_in, ht)]
    halves = (pl.ds(0, 128), pl.ds(128, 128))
    own_here = [
        bring(up.at[pl.ds(0, 4), g, :, lanes], m[name].at[pl.ds(g * 4, 4)])
        for name, lanes in zip(("a0_hold", "a1_hold"), halves)
    ]
    later = [
        bring(xh_in, m["xh"]),
        bring(wq_in.at[0], wq.at[0]),
        bring(wo_in.at[1], wo.at[1]),
        bring(wo_in.at[0], wo.at[0]),
    ]

    def held_on_line(d, s):
        t = mt[(d * 16 + gy) * 4 + s]
        return ((t >> 6) & 7) * 4 + (t & 3)

    def held_on_plane(d, s):
        return ht[g * 64 + d * 4 + s] & 63

    def back_on_line(d, s):
        return tab_s[0, d * 4 + s] & 31

    def back_on_plane(d, s):
        return tab_s[0, 64 + d * 4 + s] & 63

    def bufs(name):
        return m[name + "_hold"], m[name + "_pack"], m[name + "_got"]

    def line_exchange(name, source, code):
        return Exchange(links, links.line, g, links.on_gx, source, *bufs(name), code)

    a = [
        line_exchange(name, lambda i, p, lanes=lanes: up.at[p, i, :, lanes], held_on_line)
        for name, lanes in zip(("a0", "a1"), halves)
    ]
    b = [
        line_exchange(name, lambda i, p, name=name: m[name + "_from"].at[i, p], back_on_line)
        for name in ("b0", "b1")
    ]
    c = Exchange(
        links, links.plane, gy, links.on_gy, lambda i, p: m["c_from"].at[i, p], *bufs("c"), held_on_plane
    )
    d = Exchange(
        links, links.plane, gy, links.on_gy, lambda i, p: m["d_from"].at[i, p], *bufs("d"), back_on_plane
    )
    red1 = Reduction(links, *(m[n + "1"] for n in ("slab", "pair", "both", "red", "redx")))
    red0 = Reduction(links, *(m[n + "0"] for n in ("slab", "pair", "both", "red", "redx")))

    def put_b(t, tile):
        for i in range(8):
            m["b0_from"][i, t] = tile[16 * i : 16 * i + 16, :128]
            m["b1_from"][i, t] = tile[16 * i : 16 * i + 16, 128:]

    def put_d(t, tile):
        for i in range(16):
            lanes = slice(128 * (i % 2), 128 * (i % 2) + 128)
            m["d_from"][i, t] = tile[16 * (i // 2) : 16 * (i // 2) + 16, lanes]

    def take_a(lo, hi):
        for half in a:
            half.finish()
        for s in range(lo, hi):
            for i in range(8):
                r = s * TILE + 16 * i
                m["grad1"][r : r + 16, :128] = m["a0_got"][i, s]
                m["grad1"][r : r + 16, 128:] = m["a1_got"][i, s]

    def b_to_c(lo, hi):
        for half in b:
            half.finish()
        for s in range(lo, hi):
            for i in range(8):
                m["c_from"][2 * i, s] = m["b0_got"][i, s]
                m["c_from"][2 * i + 1, s] = m["b1_got"][i, s]
        c.spread(lo, hi)

    def take_c(lo, hi):
        c.finish()
        for s in range(lo, hi):
            for i in range(16):
                r = s * TILE + 16 * (i // 2)
                lanes = slice(128 * (i % 2), 128 * (i % 2) + 128)
                m["grad0"][r : r + 16, lanes] = m["c_got"][i, s]

    def apart(*work):
        @pl.when(g >= 0)
        def _():
            for piece in work:
                piece()

    for half in a:
        half.keep = lambda lo, hi: None
    xm_here.wait()
    gains_here.wait()
    gain0, gain1 = gains[0:1, :], gains[1:2, :]
    forward_norm(m["xm"], gain1, s1)
    links.greeted()
    for half in a:
        half.spread(0, 4)
    wq1_here.wait()
    forward_rows(wq.at[1], s1)
    for copy in lists:
        copy.wait()
    back = jnp.zeros((8, 128), jnp.int32)
    lanes = lax.broadcasted_iota(jnp.int32, (8, 128), 1)
    for j in range(32):
        t = mt[((j // 4) * 16 + gy) * 4 + j % 4]
        back = jnp.where(lanes == ((t >> 6) & 7) * 4 + (t & 3), j, back)
    for j in range(64):
        back = jnp.where(lanes == 64 + (ht[g * 64 + j] & 63), j, back)
    m["tab"][...] = back
    tab_here = bring(m["tab"], tab_s)
    apart(lambda: forward_heads(0, s1), lambda: forward_heads(1, s1))
    for copy in own_here:
        copy.wait()
    for lo in (0, 2):
        for half in a:
            half.gather(lo, lo + 2)
    for copy in later:
        copy.wait()
    apart(
        lambda: forward_norm(m["xh"], gain0, s0),
        lambda: forward_rows(wq.at[0], s0),
        lambda: forward_heads(0, s0),
        lambda: forward_heads(1, s0),
    )
    tab_here.wait()

    take_a(0, 2)
    backward_patch(0, m["grad1"], gain1, wq.at[1], wo.at[1], put_b, s1, w)
    for half in b:
        half.spread(0, 2)
    take_a(2, 4)
    backward_patch(1, m["grad1"], gain1, wq.at[1], wo.at[1], put_b, s1, w)
    for half in b:
        half.spread(2, 4)
    weight_grads(m["grad1"], s1, w, m["slab1"])
    for lo in (0, 2):
        for half in b:
            half.gather(lo, lo + 2)
    red1.partner()
    b_to_c(0, 2)
    b_to_c(2, 4)
    c.gather(0, 2)
    c.gather(2, 4)
    take_c(0, 2)
    red1.start()

    backward_patch(0, m["grad0"], gain0, wq.at[0], wo.at[0], put_d, s0, w)
    d.spread(0, 2)
    take_c(2, 4)
    backward_patch(1, m["grad0"], gain0, wq.at[0], wo.at[0], put_d, s0, w)
    d.spread(2, 4)
    weight_grads(m["grad0"], s0, w, m["slab0"])
    red0.partner()
    red1.middle()
    red0.start()
    d.gather(0, 4)
    red0.middle()
    red1.finish()
    w1_out = bring(m["redx1"], out_w.at[1])
    d.finish()
    d_out = bring(m["d_got"], out_d)
    links.drain()
    red0.finish()
    w0_out = bring(m["redx0"], out_w.at[0])
    links.drain()
    for copy in (w1_out, d_out, w0_out):
        copy.wait()


def write_out(d, sums, out, out_q, out_o, out_g):
    for s in range(4):
        for i in range(16):
            r = s * TILE + 16 * (i // 2)
            lanes = slice(128 * (i % 2), 128 * (i % 2) + 128)
            out[r : r + 16, lanes] = d[i, s]
    diagonal = lax.broadcasted_iota(jnp.int32, (16, 128), 0) == lax.broadcasted_iota(
        jnp.int32, (16, 128), 1
    )
    for b in range(2):
        low, high = (
            sum(sums[b, 2 * x + core].astype(F32) for x in range(4)) for core in (0, 1)
        )
        out_q[b, :, :HALF] = low
        out_q[b, :, HALF:] = high[:, :128]
        out_o[b] = high[:, 128:384]
        row = jnp.sum(jnp.where(diagonal, high[:, 384:512], 0.0), axis=0, keepdims=True)
        out_g[b : b + 1, :] = row[:, :16]


def per_device(up, xh, xm, gains, wq, wo, hilbert_tiles, morton_tiles):
    scratch = (
        list(BLOCK_SCRATCH.values()) * 2
        + list(WORK_SCRATCH.values())
        + list(COMM_SCRATCH.values())
    )
    vmem = pl.BlockSpec(memory_space=pltpu.VMEM)
    hbm = pl.BlockSpec(memory_space=pl.ANY)
    d, sums = pl.pallas_call(
        kernel,
        out_shape=(
            jax.ShapeDtypeStruct(PLANE, BF),
            jax.ShapeDtypeStruct((2, 8, 16, HALF), BF),
        ),
        in_specs=[hbm] * 8,
        out_specs=[hbm] * 2,
        scratch_shapes=[pltpu.VMEM(*v) for v in scratch]
        + [
            pltpu.SMEM((512,), jnp.int32),
            pltpu.SMEM((512,), jnp.int32),
            pltpu.SMEM((8, 128), jnp.int32),
        ]
        + [pltpu.SemaphoreType.DMA((N_GROUPS,))] * 2
        + [pltpu.SemaphoreType.DMA((16,))],
        compiler_params=pltpu.CompilerParams(collective_id=0, has_side_effects=True),
        name="blocks",
    )(morton_tiles, hilbert_tiles, up.reshape(4, 8, 16, C), xh, xm, gains, wq, wo)
    return pl.pallas_call(
        write_out,
        out_shape=(
            jax.ShapeDtypeStruct((512, C), BF),
            jax.ShapeDtypeStruct((2, 16, 768), F32),
            jax.ShapeDtypeStruct((2, 16, 256), F32),
            jax.ShapeDtypeStruct((2, 16), F32),
        ),
        in_specs=[vmem] * 2,
        out_specs=[vmem] * 4,
        name="write_out",
    )(d, sums)


def solution(mesh):
    rows = P(("gx", "gy"), None)
    return jax.shard_map(
        per_device,
        mesh=mesh,
        in_specs=(rows, rows, rows, P(), P(), P(), P(), P()),
        out_specs=(rows, P(None, "gy", None), P(None, "gy", None), P(None, "gy")),
        check_vma=False,
    )
```
